256 devices in a mesh: panel: 16 (over z, core), tm: 16 (over x, y).
Axes of the slice: x: 4, y: 4, z: 8, core: 2. Of those that a mesh axis runs over, the one named last changes fastest.
Arguments:
- pressures: bfloat16 [98304, 12288], P('panel', 'tm'), may hold values from -60 to 60
- sketch: bfloat16 [98304, 128], P(('panel', 'tm')), may hold values from -6 to 6
Outputs:
- basis_rows: bfloat16 [12288, 128], P('tm')
- image: float32 [98304, 128], P(('panel', 'tm'))
The draws below stay inside these ranges and needn't reach their ends.
All inputs are finite; a program needn't handle non-finite values.
Results may differ from the reference program's by a relative error of at most 0.0029.
Values may be sent and summed in bfloat16 or wider, within the bound.
No kernel may reach another device: no remote copies, remote signals or barrier semaphores. Data moves between devices by JAX's collectives and lax.ppermute only.
A program may use at most 64 MiB of HBM per device.

```python
import jax
import jax.numpy as jnp
from jax import lax

K = 128
NP = 98304
NT = 12288


def draw_pressures(key, part):
    keys = jax.random.split(key, 3)
    row_scale = jnp.exp(jax.random.uniform(keys[0], (NP, 1), jnp.float32, jnp.log(0.3), jnp.log(3.0)))
    col_scale = jnp.exp(jax.random.uniform(keys[1], (1, NT), jnp.float32, jnp.log(0.3), jnp.log(3.0)))
    base = jnp.clip(jax.random.normal(keys[2], (NP, NT), jnp.float32), -6.0, 6.0)
    return (base * row_scale * col_scale).astype(jnp.bfloat16)


def shard_levels(key, dims, pieces, least, largest):
    factor_of = 1.0
    for position, shards_of in pieces:
        steps = jax.random.uniform(jax.random.fold_in(jax.random.fold_in(key, 6), position), (shards_of,), jnp.float32, least / len(pieces), largest / len(pieces))
        factor_of = factor_of * jnp.repeat(jnp.exp(steps), dims[position] // shards_of).reshape((-1,) + (1,) * (len(dims) - 1 - position))
    return factor_of


def centred(rng, extent, deviation, bound, shards=(), held_as=jnp.bfloat16):
    drawn = deviation * jax.random.normal(rng, extent, jnp.float32)
    if shards:
        drawn = drawn * shard_levels(rng, extent, shards, -0.22, 0.18)
    return jnp.clip(drawn, -bound, bound).astype(held_as)


def setup_inputs(seed: int = 0) -> dict:
    seeds = jax.random.split(jax.random.key(seed), 3)
    return {
        "pressures": draw_pressures(jax.random.fold_in(seeds[2], 71), 0),
        "sketch": centred(seeds[1], (NP, K), 1.0, 6.0, ((0, 256),)),
    }


def reference(pressures, sketch):
    y_full = lax.dot_general(pressures.astype(jnp.float32), sketch.astype(jnp.float32), (((0,), (0,)), ((), ())), preferred_element_type=jnp.float32)
    gram_matrix = lax.dot_general(y_full.astype(jnp.float32), y_full.astype(jnp.float32), (((0,), (0,)), ((), ())), precision=lax.Precision.HIGHEST, preferred_element_type=jnp.float32)
    lower_factor = jnp.linalg.cholesky(gram_matrix)
    solved = jax.scipy.linalg.solve_triangular(lower_factor, y_full.T, lower=True)
    basis_rows = solved.T.astype(jnp.bfloat16)
    image = jnp.dot(pressures.astype(jnp.float32), basis_rows.astype(jnp.float32), preferred_element_type=jnp.float32)
    return (basis_rows, image)
```

```python
import jax
import jax.numpy as jnp
from jax import lax
from jax.sharding import PartitionSpec as P

F32 = jnp.float32
BF16 = jnp.bfloat16


def spread(block, axis):
    size = lax.axis_size(axis)
    return lax.all_to_all(jnp.broadcast_to(block[None], (size, *block.shape)), axis, 0, 0)


def sum_scattered(rows, axis, sent_as):
    size = lax.axis_size(axis)
    parts = rows.reshape(size, rows.shape[0] // size, rows.shape[1]).astype(sent_as)
    return jnp.sum(lax.all_to_all(parts, axis, 0, 0).astype(F32), axis=0)


def gram_of(rows_block):
    return lax.dot_general(
        rows_block,
        rows_block,
        (((0,), (0,)), ((), ())),
        precision=lax.Precision.HIGHEST,
        preferred_element_type=F32,
    )


def gram_summed(y_rows):
    partial = gram_of(y_rows)
    modes = partial.shape[0]
    core = lax.axis_index("panel") % 2
    half = lax.dynamic_slice_in_dim(partial, core * (modes // 2), modes // 2, 0)
    mine = jnp.sum(spread(half, "tm"), axis=0)
    other = lax.ppermute(mine, "panel", [(i, i ^ 1) for i in range(lax.axis_size("panel"))])
    low = jnp.where(core == 0, mine, other)
    high = jnp.where(core == 0, other, mine)
    return jnp.concatenate([low, high], axis=0)


def orthonormal(rows_block, gram_matrix):
    lower_factor = jnp.linalg.cholesky(gram_matrix)
    solved = jax.scipy.linalg.solve_triangular(lower_factor, rows_block.T, lower=True)
    return solved.T.astype(BF16)


def on_device(pressures, sketch):
    panels, samples = pressures.shape
    modes = sketch.shape[1]
    partial_y = lax.dot_general(
        pressures,
        spread(sketch, "tm").reshape(panels, modes),
        (((0,), (0,)), ((), ())),
        preferred_element_type=F32,
    )
    y_rows = spread(sum_scattered(partial_y, "panel", F32), "panel").reshape(samples, modes)
    basis_rows = orthonormal(y_rows, gram_summed(y_rows))
    partial_image = jnp.dot(pressures, basis_rows, preferred_element_type=F32)
    image = sum_scattered(partial_image, "tm", BF16)
    return (basis_rows, image)


def solution(mesh):
    return jax.shard_map(
        on_device,
        mesh=mesh,
        in_specs=(P("panel", "tm"), P(("panel", "tm"), None)),
        out_specs=(P("tm", None), P(("panel", "tm"), None)),
        check_vma=False,
    )
```

```python
import jax
import jax.numpy as jnp
from jax import lax
from jax.experimental import pallas as pl
from jax.experimental.pallas import tpu as pltpu
from jax.sharding import PartitionSpec as P

F32 = jnp.float32
BF16 = jnp.bfloat16
GROUP = 8
PIECES = 6
IN_HBM = pl.BlockSpec(memory_space=pltpu.HBM)
IN_VMEM = pl.BlockSpec(memory_space=pltpu.VMEM)
ROOM = pltpu.CompilerParams(vmem_limit_bytes=32 << 20)


def spread(block, axis):
    size = lax.axis_size(axis)
    return lax.all_to_all(jnp.broadcast_to(block[None], (size, *block.shape)), axis, 0, 0)


def fetch(pressures, held, arrived):
    rows = held.shape[0] // PIECES
    parts = [pl.ds(i * rows, rows) for i in range(PIECES)]
    copies = [pltpu.make_async_copy(pressures.at[r], held.at[r], arrived.at[i]) for i, r in enumerate(parts)]
    for copy in copies:
        copy.start()
    return list(zip(copies, parts))


def held_like(pressures):
    return [pltpu.VMEM(pressures.shape, pressures.dtype), pltpu.SemaphoreType.DMA((PIECES,))]


def projection_kernel(pressures, sketch, y_ref, held, arrived):
    total = None
    for copy, r in fetch(pressures, held, arrived):
        copy.wait()
        term = lax.dot_general(sketch[r, :], held[r, :], (((0,), (0,)), ((), ())), preferred_element_type=F32)
        total = term if total is None else total + term
    y_ref[...] = total.T


def projection(pressures, sketch):
    panels, samples = pressures.shape
    modes = sketch.shape[1]
    return pl.pallas_call(
        projection_kernel,
        out_shape=jax.ShapeDtypeStruct((samples, modes), F32),
        in_specs=[IN_HBM, IN_VMEM],
        out_specs=IN_VMEM,
        scratch_shapes=held_like(pressures),
        compiler_params=ROOM,
    )(pressures, sketch)


def inverse_factor(gram):
    n = gram.shape[0]
    groups = n // GROUP
    sub = lax.broadcasted_iota(jnp.int32, (GROUP, n), 0)
    lane = lax.broadcasted_iota(jnp.int32, (GROUP, n), 1)

    def wide(x):
        return jnp.broadcast_to(x, (GROUP, n))

    left = [gram[GROUP * i : GROUP * (i + 1), :] for i in range(groups)]
    right = [jnp.where(lane == sub + GROUP * i, 1.0, 0.0).astype(F32) for i in range(groups)]
    steps = range(GROUP)
    for g in range(groups):
        k = GROUP * g
        columns = [wide(left[g][:, k + m : k + m + 1]) for m in steps]
        block = {(m, l): columns[l][m : m + 1, :] for m in steps for l in range(m, GROUP)}
        over, scale = [], {}
        for m in steps:
            over.append(1.0 / block[m, m])
            for l in range(m + 1, GROUP):
                scale[m, l] = block[m, l] * over[m]
            for p in range(m + 1, GROUP):
                for l in range(p, GROUP):
                    block[p, l] = block[p, l] - scale[m, p] * block[m, l]
        rows_left, rows_right = [], []
        for m in steps:
            a, b = left[g][m : m + 1, :], right[g][m : m + 1, :]
            for l in range(m):
                a = a - scale[l, m] * rows_left[l]
                b = b - scale[l, m] * rows_right[l]
            rows_left.append(a)
            rows_right.append(b)
        pivot_left = [wide(rows_left[m] * over[m]) for m in steps]
        pivot_right = [wide(rows_right[m] * over[m]) for m in steps]
        scales = {key: wide(value) for key, value in scale.items()}
        for i in range(g, groups):
            own = i == g
            entries = columns if own else [wide(left[i][:, k + m : k + m + 1]) for m in steps]
            factors = []
            for m in steps:
                f = entries[m]
                for l in range(m):
                    f = f - scales[l, m] * factors[l]
                factors.append(f)
            a, b = left[i], right[i]
            for m in range(GROUP - 1) if own else steps:
                f = jnp.where(sub > m, factors[m], 0.0) if own else factors[m]
                a = a - f * pivot_left[m]
                b = b - f * pivot_right[m]
            left[i], right[i] = a, b
    out = []
    for i in range(groups):
        pivots = jnp.sum(jnp.where(lane == sub + GROUP * i, left[i], 0.0), axis=1, keepdims=True)
        root = lax.rsqrt(pivots)
        root = root * (1.5 - 0.5 * pivots * root * root)
        out.append(right[i] * root)
    return out


def image_kernel(core, pressures, mine, other, y_ref, basis_ref, image_ref, held, arrived, inverse):
    arriving = fetch(pressures, held, arrived)
    first = core[0] == 0
    low = jnp.where(first, mine[...], other[...])
    high = jnp.where(first, other[...], mine[...])
    for i, rows in enumerate(inverse_factor(jnp.concatenate([low, high], axis=0))):
        inverse[GROUP * i : GROUP * (i + 1), :] = rows
    basis = lax.dot_general(
        y_ref[...],
        inverse[...],
        (((1,), (1,)), ((), ())),
        precision=lax.Precision.HIGHEST,
        preferred_element_type=F32,
    ).astype(BF16)
    basis_ref[...] = basis
    for copy, r in arriving:
        copy.wait()
        image_ref[r, :] = jnp.dot(held[r, :], basis, preferred_element_type=F32).astype(BF16)


def basis_and_image(core, pressures, mine, other, y_rows):
    panels = pressures.shape[0]
    samples, modes = y_rows.shape
    return pl.pallas_call(
        image_kernel,
        out_shape=(
            jax.ShapeDtypeStruct((samples, modes), BF16),
            jax.ShapeDtypeStruct((panels, modes), BF16),
        ),
        in_specs=[pl.BlockSpec(memory_space=pltpu.SMEM), IN_HBM, IN_VMEM, IN_VMEM, IN_VMEM],
        out_specs=(IN_VMEM, IN_VMEM),
        scratch_shapes=[*held_like(pressures), pltpu.VMEM((modes, modes), F32)],
        compiler_params=ROOM,
    )(core[None], pressures, mine, other, y_rows)


def gram_half(y_rows, core):
    gram = lax.dot_general(
        y_rows,
        y_rows,
        (((0,), (0,)), ((), ())),
        precision=lax.Precision.HIGHEST,
        preferred_element_type=F32,
    )
    half = gram.shape[0] // 2
    return lax.dynamic_slice_in_dim(gram, core * half, half, 0)


def on_device(pressures, sketch):
    pressures = pltpu.with_memory_space_constraint(pressures, pltpu.HBM)
    panels, samples = pressures.shape
    modes = sketch.shape[1]
    across = lax.axis_size("panel")
    core = lax.axis_index("panel") % 2
    partial_y = projection(pressures, spread(sketch, "tm").reshape(panels, modes))
    pieces = lax.all_to_all(partial_y.reshape(across, samples // across, modes), "panel", 0, 0)
    y_rows = spread(jnp.sum(pieces, axis=0), "panel").reshape(samples, modes)
    mine = jnp.sum(spread(gram_half(y_rows, core), "tm"), axis=0)
    other = lax.ppermute(mine, "panel", [(i, i ^ 1) for i in range(across)])
    basis_rows, partial_image = basis_and_image(core, pressures, mine, other, y_rows)
    parts = lax.all_to_all(partial_image.reshape(lax.axis_size("tm"), -1, modes), "tm", 0, 0)
    image = jnp.sum(parts.astype(F32), axis=0)
    return (basis_rows, image)


def solution(mesh):
    return jax.shard_map(
        on_device,
        mesh=mesh,
        in_specs=(P("panel", "tm"), P(("panel", "tm"), None)),
        out_specs=(P("tm", None), P(("panel", "tm"), None)),
        check_vma=False,
    )
```

```python
import jax
import jax.numpy as jnp
from jax import lax
from jax.experimental import pallas as pl
from jax.experimental.pallas import tpu as pltpu
from jax.sharding import PartitionSpec as P

F32 = jnp.float32
BF16 = jnp.bfloat16
GROUP = 8
PIECES = 6
IN_HBM = pl.BlockSpec(memory_space=pltpu.HBM)
IN_VMEM = pl.BlockSpec(memory_space=pltpu.VMEM)
ROOM = pltpu.CompilerParams(vmem_limit_bytes=32 << 20)


def fetch(pressures, held, arrived):
    rows = held.shape[0] // PIECES
    parts = [pl.ds(i * rows, rows) for i in range(PIECES)]
    copies = [pltpu.make_async_copy(pressures.at[r], held.at[r], arrived.at[i]) for i, r in enumerate(parts)]
    for copy in copies:
        copy.start()
    return list(zip(copies, parts))


def held_like(pressures):
    return [pltpu.VMEM(pressures.shape, pressures.dtype), pltpu.SemaphoreType.DMA((PIECES,))]


def own_core():
    return lax.rem(lax.axis_index("panel"), 2)


def projection_kernel(pressures, sketch, keep_ref, give_ref, held, arrived):
    total = None
    for copy, r in fetch(pressures, held, arrived):
        copy.wait()
        term = lax.dot_general(sketch[r, :], held[r, :], (((0,), (0,)), ((), ())), preferred_element_type=F32)
        total = term if total is None else total + term
    chips, rows, modes = keep_ref.shape
    y = total.T.reshape(chips, 2, rows, modes)
    first = own_core() == 0
    keep_ref[...] = jnp.where(first, y[:, 0], y[:, 1])
    give_ref[...] = jnp.where(first, y[:, 1], y[:, 0])


def projection(pressures, sketch, chips):
    samples = pressures.shape[1]
    modes = sketch.shape[1]
    half = jax.ShapeDtypeStruct((chips, samples // (2 * chips), modes), F32)
    return pl.pallas_call(
        projection_kernel,
        out_shape=(half, half),
        in_specs=[IN_HBM, IN_VMEM],
        out_specs=(IN_VMEM, IN_VMEM),
        scratch_shapes=held_like(pressures),
        compiler_params=ROOM,
    )(pressures, sketch)


def gram_kernel(mine, other, y_ref, half_ref):
    first = own_core() == 0
    y_ref[:, 0] = jnp.where(first, mine[...], other[...])
    y_ref[:, 1] = jnp.where(first, other[...], mine[...])
    copies, half, modes = half_ref.shape
    y = y_ref[...].reshape(-1, modes)
    gram = lax.dot_general(
        y, y, (((0,), (0,)), ((), ())), precision=lax.Precision.HIGHEST, preferred_element_type=F32
    )
    half_ref[...] = jnp.broadcast_to(jnp.where(first, gram[:half], gram[half:])[None], half_ref.shape)


def rows_and_gram(mine, other, copies):
    chips, rows, modes = mine.shape
    return pl.pallas_call(
        gram_kernel,
        out_shape=(
            jax.ShapeDtypeStruct((chips, 2, rows, modes), F32),
            jax.ShapeDtypeStruct((copies, modes // 2, modes), F32),
        ),
        in_specs=[IN_VMEM, IN_VMEM],
        out_specs=(IN_VMEM, IN_VMEM),
        compiler_params=ROOM,
    )(mine, other)


def inverse_factor(gram):
    n = gram.shape[0]
    groups = n // GROUP
    sub = lax.broadcasted_iota(jnp.int32, (GROUP, n), 0)
    lane = lax.broadcasted_iota(jnp.int32, (GROUP, n), 1)
    steps = range(GROUP)

    def wide(x):
        return jnp.broadcast_to(x, (GROUP, n))

    def columns_of(rows, k):
        return [wide(rows[:, k + m : k + m + 1]) for m in steps]

    left = [gram[GROUP * i : GROUP * (i + 1), :] for i in range(groups)]
    out = []
    for g in range(groups):
        k = GROUP * g
        inside = (lane >= k) & (lane < k + GROUP)
        columns = columns_of(left[g], k)
        block = {(m, l): columns[l][m : m + 1, :] for m in steps for l in range(m, GROUP)}
        over, scale = [], {}
        for m in steps:
            over.append(1.0 / block[m, m])
            for l in range(m + 1, GROUP):
                scale[m, l] = block[m, l] * over[m]
            for p in range(m + 1, GROUP):
                for l in range(p, GROUP):
                    block[p, l] = block[p, l] - scale[m, p] * block[m, l]
        start = jnp.where(inside, jnp.where(lane == sub + k, 1.0, 0.0), left[g])
        rows = []
        for m in steps:
            row = start[m : m + 1, :]
            for l in range(m):
                row = row - scale[l, m] * rows[l]
            rows.append(row)
        pivots = [wide(rows[m] * over[m]) for m in steps]
        scales = {key: wide(value) for key, value in scale.items()}
        for i in range(g + 1, groups):
            factors = []
            for m, f in enumerate(columns_of(left[i], k)):
                for l in range(m):
                    f = f - scales[l, m] * factors[l]
                factors.append(f)
            rest = jnp.where(inside, 0.0, left[i])
            for f, pivot in zip(factors, pivots):
                rest = rest - f * pivot
            left[i] = rest
        scaled = []
        for m in steps:
            root = lax.rsqrt(block[m, m])
            scaled.append(rows[m] * (root * (1.5 - 0.5 * block[m, m] * root * root)))
        out.append(jnp.where(lane < k + GROUP, jnp.concatenate(scaled, axis=0), 0.0))
    return out


def image_kernel(pressures, mine, other, y_ref, basis_ref, image_ref, held, arrived, inverse):
    arriving = fetch(pressures, held, arrived)
    first = own_core() == 0
    low = jnp.where(first, mine[...], other[...])
    high = jnp.where(first, other[...], mine[...])
    for i, rows in enumerate(inverse_factor(jnp.concatenate([low, high], axis=0))):
        inverse[GROUP * i : GROUP * (i + 1), :] = rows
    basis = lax.dot_general(
        y_ref[...],
        inverse[...],
        (((1,), (1,)), ((), ())),
        precision=lax.Precision.HIGHEST,
        preferred_element_type=F32,
    ).astype(BF16)
    basis_ref[...] = basis
    for copy, r in arriving:
        copy.wait()
        image_ref[r, :] = jnp.dot(held[r, :], basis, preferred_element_type=F32).astype(BF16)


def basis_and_image(pressures, mine, other, y_rows):
    panels = pressures.shape[0]
    samples, modes = y_rows.shape
    return pl.pallas_call(
        image_kernel,
        out_shape=(
            jax.ShapeDtypeStruct((samples, modes), BF16),
            jax.ShapeDtypeStruct((panels, modes), BF16),
        ),
        in_specs=[IN_HBM, IN_VMEM, IN_VMEM, IN_VMEM],
        out_specs=(IN_VMEM, IN_VMEM),
        scratch_shapes=[*held_like(pressures), pltpu.VMEM((modes, modes), F32)],
        compiler_params=ROOM,
    )(pressures, mine, other, y_rows)


def swap_cores(x):
    return lax.ppermute(x, "panel", [(i, i ^ 1) for i in range(lax.axis_size("panel"))])


def exchange(x, axis, groups=None):
    return lax.all_to_all(x, axis, 0, 0, axis_index_groups=groups)


def on_device(pressures, sketch):
    pressures = pltpu.with_memory_space_constraint(pressures, pltpu.HBM)
    panels, samples = pressures.shape
    modes = sketch.shape[1]
    blocks = lax.axis_size("tm")
    chips = lax.axis_size("panel") // 2
    same_core = [[2 * z + c for z in range(chips)] for c in range(2)]

    gathered = exchange(jnp.broadcast_to(sketch[None], (blocks, *sketch.shape)), "tm")
    keep, give = projection(pressures, gathered.reshape(panels, modes), chips)
    own = jnp.sum(exchange(keep + swap_cores(give), "panel", same_core), axis=0)
    mine = exchange(jnp.broadcast_to(own[None], (chips, *own.shape)), "panel", same_core)
    y_rows, half = rows_and_gram(mine, swap_cores(mine), blocks)
    half = jnp.sum(exchange(half, "tm"), axis=0)
    basis_rows, partial_image = basis_and_image(
        pressures, half, swap_cores(half), y_rows.reshape(samples, modes)
    )
    image = jnp.sum(exchange(partial_image.reshape(blocks, -1, modes), "tm").astype(F32), axis=0)
    return (basis_rows, image)


def solution(mesh):
    return jax.shard_map(
        on_device,
        mesh=mesh,
        in_specs=(P("panel", "tm"), P(("panel", "tm"), None)),
        out_specs=(P("tm", None), P(("panel", "tm"), None)),
        check_vma=False,
    )
```

```python
import math

import jax
import jax.numpy as jnp
from jax import lax
from jax.experimental import pallas as pl
from jax.experimental.pallas import tpu as pltpu
from jax.sharding import PartitionSpec as P

F32 = jnp.float32
BF16 = jnp.bfloat16
GROUP = 8
PIECES = 6
IN_HBM = pl.BlockSpec(memory_space=pltpu.HBM)
IN_VMEM = pl.BlockSpec(memory_space=pltpu.VMEM)
ROOM = pltpu.CompilerParams(vmem_limit_bytes=32 << 20)


def fetch(pressures, held, arrived):
    rows = held.shape[0] // PIECES
    parts = [pl.ds(i * rows, rows) for i in range(PIECES)]
    copies = [pltpu.make_async_copy(pressures.at[r], held.at[r], arrived.at[i]) for i, r in enumerate(parts)]
    for copy in copies:
        copy.start()
    return list(zip(copies, parts))


def held_like(pressures):
    return [pltpu.VMEM(pressures.shape, pressures.dtype), pltpu.SemaphoreType.DMA((PIECES,))]


def own_core():
    return lax.rem(lax.axis_index("panel"), 2)


def projection_kernel(pressures, sketch, keep_ref, give_ref, held, arrived):
    total = None
    for copy, r in fetch(pressures, held, arrived):
        copy.wait()
        term = lax.dot_general(sketch[r, :], held[r, :], (((0,), (0,)), ((), ())), preferred_element_type=F32)
        total = term if total is None else total + term
    chips, rows, modes = keep_ref.shape
    y = total.T.reshape(chips, 2, rows, modes)
    first = own_core() == 0
    keep_ref[...] = jnp.where(first, y[:, 0], y[:, 1])
    give_ref[...] = jnp.where(first, y[:, 1], y[:, 0])


def projection(pressures, sketch, chips):
    samples = pressures.shape[1]
    modes = sketch.shape[1]
    half = jax.ShapeDtypeStruct((chips, samples // (2 * chips), modes), F32)
    return pl.pallas_call(
        projection_kernel,
        out_shape=(half, half),
        in_specs=[IN_HBM, IN_VMEM],
        out_specs=(IN_VMEM, IN_VMEM),
        scratch_shapes=held_like(pressures),
        compiler_params=ROOM,
    )(pressures, sketch)


def gram_kernel(mine, other, y_ref, copies_ref):
    first = own_core() == 0
    y_ref[:, 0] = jnp.where(first, mine[...], other[...])
    y_ref[:, 1] = jnp.where(first, other[...], mine[...])
    y = y_ref[...].reshape(-1, y_ref.shape[3])
    gram = lax.dot_general(
        y, y, (((0,), (0,)), ((), ())), precision=lax.Precision.HIGHEST, preferred_element_type=F32
    )
    copies_ref[...] = jnp.broadcast_to(gram[None], copies_ref.shape)


def rows_and_gram(mine, other, copies):
    chips, rows, modes = mine.shape
    return pl.pallas_call(
        gram_kernel,
        out_shape=(
            jax.ShapeDtypeStruct((chips, 2, rows, modes), F32),
            jax.ShapeDtypeStruct((copies, modes, modes), F32),
        ),
        in_specs=[IN_VMEM, IN_VMEM],
        out_specs=(IN_VMEM, IN_VMEM),
        compiler_params=ROOM,
    )(mine, other)


def inverse_factor(gram):
    n = gram.shape[0]
    groups = n // GROUP
    sub = lax.broadcasted_iota(jnp.int32, (GROUP, n), 0)
    lane = lax.broadcasted_iota(jnp.int32, (GROUP, n), 1)
    steps = range(GROUP)

    def wide(x):
        return jnp.broadcast_to(x, (GROUP, n))

    def columns_of(rows, k):
        return [wide(rows[:, k + m : k + m + 1]) for m in steps]

    left = [gram[GROUP * i : GROUP * (i + 1), :] for i in range(groups)]
    out = []
    for g in range(groups):
        k = GROUP * g
        inside = (lane >= k) & (lane < k + GROUP)
        columns = columns_of(left[g], k)
        block = {(m, l): columns[l][m : m + 1, :] for m in steps for l in range(m, GROUP)}
        over, scale = [], {}
        for m in steps:
            over.append(1.0 / block[m, m])
            for l in range(m + 1, GROUP):
                scale[m, l] = block[m, l] * over[m]
            for p in range(m + 1, GROUP):
                for l in range(p, GROUP):
                    block[p, l] = block[p, l] - scale[m, p] * block[m, l]
        start = jnp.where(inside, jnp.where(lane == sub + k, 1.0, 0.0), left[g])
        rows = []
        for m in steps:
            row = start[m : m + 1, :]
            for l in range(m):
                row = row - scale[l, m] * rows[l]
            rows.append(row)
        pivots = [wide(rows[m] * over[m]) for m in steps]
        scales = {key: wide(value) for key, value in scale.items()}
        for i in range(g + 1, groups):
            factors = []
            for m, f in enumerate(columns_of(left[i], k)):
                for l in range(m):
                    f = f - scales[l, m] * factors[l]
                factors.append(f)
            rest = jnp.where(inside, 0.0, left[i])
            for f, pivot in zip(factors, pivots):
                rest = rest - f * pivot
            left[i] = rest
        scaled = []
        for m in steps:
            root = lax.rsqrt(block[m, m])
            scaled.append(rows[m] * (root * (1.5 - 0.5 * block[m, m] * root * root)))
        out.append(jnp.where(lane < k + GROUP, jnp.concatenate(scaled, axis=0), 0.0))
    return out


def image_kernel(pressures, gram_parts, y_ref, basis_ref, image_ref, held, arrived, inverse):
    arriving = fetch(pressures, held, arrived)
    for i, rows in enumerate(inverse_factor(jnp.sum(gram_parts[...], axis=0))):
        inverse[GROUP * i : GROUP * (i + 1), :] = rows
    basis = lax.dot_general(
        y_ref[...],
        inverse[...],
        (((1,), (1,)), ((), ())),
        precision=lax.Precision.HIGHEST,
        preferred_element_type=F32,
    ).astype(BF16)
    basis_ref[...] = basis
    for copy, r in arriving:
        copy.wait()
        image_ref[r, :] = jnp.dot(held[r, :], basis, preferred_element_type=F32).astype(BF16)


def basis_and_image(pressures, gram_parts, y_rows):
    panels = pressures.shape[0]
    samples, modes = y_rows.shape
    return pl.pallas_call(
        image_kernel,
        out_shape=(
            jax.ShapeDtypeStruct((samples, modes), BF16),
            jax.ShapeDtypeStruct((panels, modes), BF16),
        ),
        in_specs=[IN_HBM, IN_VMEM, IN_VMEM],
        out_specs=(IN_VMEM, IN_VMEM),
        scratch_shapes=[*held_like(pressures), pltpu.VMEM((modes, modes), F32)],
        compiler_params=ROOM,
    )(pressures, gram_parts, y_rows)


def swap_cores(x):
    return lax.ppermute(x, "panel", [(i, i ^ 1) for i in range(lax.axis_size("panel"))])


def exchange(x, axis, groups=None):
    return lax.all_to_all(x, axis, 0, 0, axis_index_groups=groups)


def on_device(pressures, sketch):
    pressures = pltpu.with_memory_space_constraint(pressures, pltpu.HBM)
    panels, samples = pressures.shape
    modes = sketch.shape[1]
    blocks = lax.axis_size("tm")
    chips = lax.axis_size("panel") // 2
    side = math.isqrt(blocks)
    same_x = [[x * side + y for y in range(side)] for x in range(side)]
    same_y = [[x * side + y for x in range(side)] for y in range(side)]
    same_core = [[2 * z + c for z in range(chips)] for c in range(2)]

    gathered = exchange(jnp.broadcast_to(sketch[None], (blocks, *sketch.shape)), "tm")
    keep, give = projection(pressures, gathered.reshape(panels, modes), chips)
    own = jnp.sum(exchange(keep + swap_cores(give), "panel", same_core), axis=0)
    mine = exchange(jnp.broadcast_to(own[None], (chips, *own.shape)), "panel", same_core)
    y_rows, gram = rows_and_gram(mine, swap_cores(mine), side)
    line = jnp.sum(exchange(gram, "tm", same_x), axis=0)
    gram_parts = exchange(jnp.broadcast_to(line[None], gram.shape), "tm", same_y)
    basis_rows, partial_image = basis_and_image(pressures, gram_parts, y_rows.reshape(samples, modes))
    image = jnp.sum(exchange(partial_image.reshape(blocks, -1, modes), "tm").astype(F32), axis=0)
    return (basis_rows, image)


def solution(mesh):
    return jax.shard_map(
        on_device,
        mesh=mesh,
        in_specs=(P("panel", "tm"), P(("panel", "tm"), None)),
        out_specs=(P("tm", None), P(("panel", "tm"), None)),
        check_vma=False,
    )
```

```python
import functools
import math

import jax
import jax.numpy as jnp
from jax import lax
from jax.experimental import pallas as pl
from jax.experimental.pallas import tpu as pltpu
from jax.sharding import PartitionSpec as P

F32 = jnp.float32
BF16 = jnp.bfloat16
GROUP = 8
PIECES = 6
IN_HBM = pl.BlockSpec(memory_space=pltpu.HBM)
IN_VMEM = pl.BlockSpec(memory_space=pltpu.VMEM)
ROOM = pltpu.CompilerParams(vmem_limit_bytes=32 << 20)


def own_core():
    return lax.rem(lax.axis_index("panel"), 2)


def fetch(pressures, held, arrived, sources):
    rows = held.shape[0] // len(sources)
    copies, parts = [], []
    for i, source in enumerate(sources):
        start = source * rows if isinstance(source, int) else pl.multiple_of(source * rows, rows)
        parts.append(pl.ds(i * rows, rows))
        copies.append(pltpu.make_async_copy(pressures.at[pl.ds(start, rows)], held.at[parts[-1]], arrived.at[i]))
    for copy in copies:
        copy.start()
    return list(zip(copies, parts))


def held_like(pressures, pieces):
    return [pltpu.VMEM(pressures.shape, pressures.dtype), pltpu.SemaphoreType.DMA((pieces,))]


def projection_kernel(side, pressures, sketch, keep_ref, give_ref, held, arrived):
    first = own_core() == 0
    blocks = [(a, b) for a in range(side) for b in range(side)]
    sources = [jnp.where(first, a * side + b, b * side + a) for a, b in blocks]
    arriving = fetch(pressures, held, arrived, sources)
    total = None
    for i in range(0, len(arriving), side):
        for copy, _ in arriving[i : i + side]:
            copy.wait()
        rows = side * (held.shape[0] // len(blocks))
        r = pl.ds((i // side) * rows, rows)
        term = lax.dot_general(sketch[r, :], held[r, :], (((0,), (0,)), ((), ())), preferred_element_type=F32)
        total = term if total is None else total + term
    chips, rows, modes = keep_ref.shape
    y = total.T.reshape(chips, 2, rows, modes)
    keep_ref[...] = jnp.where(first, y[:, 0], y[:, 1])
    give_ref[...] = jnp.where(first, y[:, 1], y[:, 0])


def projection(pressures, sketch, chips, side):
    samples = pressures.shape[1]
    modes = sketch.shape[1]
    half = jax.ShapeDtypeStruct((chips, samples // (2 * chips), modes), F32)
    return pl.pallas_call(
        functools.partial(projection_kernel, side),
        out_shape=(half, half),
        in_specs=[IN_HBM, IN_VMEM],
        out_specs=(IN_VMEM, IN_VMEM),
        scratch_shapes=held_like(pressures, side * side),
        compiler_params=ROOM,
    )(pressures, sketch)


def gram_kernel(mine, other, y_ref, copies_ref):
    first = own_core() == 0
    y_ref[:, 0] = jnp.where(first, mine[...], other[...])
    y_ref[:, 1] = jnp.where(first, other[...], mine[...])
    y = y_ref[...].reshape(-1, y_ref.shape[3])
    gram = lax.dot_general(
        y, y, (((0,), (0,)), ((), ())), precision=lax.Precision.HIGHEST, preferred_element_type=F32
    )
    copies_ref[...] = jnp.broadcast_to(gram[None], copies_ref.shape)


def rows_and_gram(mine, other, copies):
    chips, rows, modes = mine.shape
    return pl.pallas_call(
        gram_kernel,
        out_shape=(
            jax.ShapeDtypeStruct((chips, 2, rows, modes), F32),
            jax.ShapeDtypeStruct((copies, modes, modes), F32),
        ),
        in_specs=[IN_VMEM, IN_VMEM],
        out_specs=(IN_VMEM, IN_VMEM),
        compiler_params=ROOM,
    )(mine, other)


def inverse_factor(gram):
    n = gram.shape[0]
    groups = n // GROUP
    sub = lax.broadcasted_iota(jnp.int32, (GROUP, n), 0)
    lane = lax.broadcasted_iota(jnp.int32, (GROUP, n), 1)
    steps = range(GROUP)

    def wide(x):
        return jnp.broadcast_to(x, (GROUP, n))

    def columns_of(rows, k):
        return [wide(rows[:, k + m : k + m + 1]) for m in steps]

    left = [gram[GROUP * i : GROUP * (i + 1), :] for i in range(groups)]
    out = []
    for g in range(groups):
        k = GROUP * g
        inside = (lane >= k) & (lane < k + GROUP)
        columns = columns_of(left[g], k)
        block = {(m, l): columns[l][m : m + 1, :] for m in steps for l in range(m, GROUP)}
        over, scale = [], {}
        for m in steps:
            over.append(1.0 / block[m, m])
            for l in range(m + 1, GROUP):
                scale[m, l] = block[m, l] * over[m]
            for p in range(m + 1, GROUP):
                for l in range(p, GROUP):
                    block[p, l] = block[p, l] - scale[m, p] * block[m, l]
        start = jnp.where(inside, jnp.where(lane == sub + k, 1.0, 0.0), left[g])
        rows = []
        for m in steps:
            row = start[m : m + 1, :]
            for l in range(m):
                row = row - scale[l, m] * rows[l]
            rows.append(row)
        pivots = [wide(rows[m] * over[m]) for m in steps]
        scales = {key: wide(value) for key, value in scale.items()}
        for i in range(g + 1, groups):
            factors = []
            for m, f in enumerate(columns_of(left[i], k)):
                for l in range(m):
                    f = f - scales[l, m] * factors[l]
                factors.append(f)
            rest = jnp.where(inside, 0.0, left[i])
            for f, pivot in zip(factors, pivots):
                rest = rest - f * pivot
            left[i] = rest
        scaled = []
        for m in steps:
            root = lax.rsqrt(block[m, m])
            scaled.append(rows[m] * (root * (1.5 - 0.5 * block[m, m] * root * root)))
        out.append(jnp.where(lane < k + GROUP, jnp.concatenate(scaled, axis=0), 0.0))
    return out


def image_kernel(pressures, gram_parts, y_ref, basis_ref, image_ref, held, arrived, inverse):
    arriving = fetch(pressures, held, arrived, range(PIECES))
    for i, rows in enumerate(inverse_factor(jnp.sum(gram_parts[...], axis=0))):
        inverse[GROUP * i : GROUP * (i + 1), :] = rows
    basis = lax.dot_general(
        y_ref[...],
        inverse[...],
        (((1,), (1,)), ((), ())),
        precision=lax.Precision.HIGHEST,
        preferred_element_type=F32,
    ).astype(BF16)
    basis_ref[...] = basis
    for copy, r in arriving:
        copy.wait()
        image_ref[r, :] = jnp.dot(held[r, :], basis, preferred_element_type=F32).astype(BF16)


def basis_and_image(pressures, gram_parts, y_rows):
    panels = pressures.shape[0]
    samples, modes = y_rows.shape
    return pl.pallas_call(
        image_kernel,
        out_shape=(
            jax.ShapeDtypeStruct((samples, modes), BF16),
            jax.ShapeDtypeStruct((panels, modes), BF16),
        ),
        in_specs=[IN_HBM, IN_VMEM, IN_VMEM],
        out_specs=(IN_VMEM, IN_VMEM),
        scratch_shapes=[*held_like(pressures, PIECES), pltpu.VMEM((modes, modes), F32)],
        compiler_params=ROOM,
    )(pressures, gram_parts, y_rows)


def swap_cores(x):
    return lax.ppermute(x, "panel", [(i, i ^ 1) for i in range(lax.axis_size("panel"))])


def exchange(x, axis, groups=None):
    return lax.all_to_all(x, axis, 0, 0, axis_index_groups=groups)


def turns(across, side):
    along = [[], []]
    for p in range(across):
        at = [[p * side * side + x * side + y for y in range(side)] for x in range(side)]
        lines = [at, [list(column) for column in zip(*at)]]
        for turn in range(2):
            along[turn] += lines[(p + turn) % 2]
    return along


def copies_of(x, count):
    return jnp.broadcast_to(x[None], (count, *x.shape))


def on_device(pressures, sketch):
    pressures = pltpu.with_memory_space_constraint(pressures, pltpu.HBM)
    panels, samples = pressures.shape
    modes = sketch.shape[1]
    blocks = lax.axis_size("tm")
    across = lax.axis_size("panel")
    chips = across // 2
    side = math.isqrt(blocks)
    same_x = [[x * side + y for y in range(side)] for x in range(side)]
    same_y = [[x * side + y for x in range(side)] for y in range(side)]
    same_core = [[2 * z + c for z in range(chips)] for c in range(2)]
    one_way, other_way = turns(across, side)

    line = exchange(copies_of(sketch, side), ("panel", "tm"), one_way)
    gathered = exchange(copies_of(line, side), ("panel", "tm"), other_way)
    keep, give = projection(pressures, gathered.reshape(panels, modes), chips, side)
    own = jnp.sum(exchange(keep + swap_cores(give), "panel", same_core), axis=0)
    mine = exchange(copies_of(own, chips), "panel", same_core)
    y_rows, gram = rows_and_gram(mine, swap_cores(mine), side)
    line = jnp.sum(exchange(gram, "tm", same_x), axis=0)
    gram_parts = exchange(copies_of(line, side), "tm", same_y)
    basis_rows, partial_image = basis_and_image(pressures, gram_parts, y_rows.reshape(samples, modes))
    image = jnp.sum(exchange(partial_image.reshape(blocks, -1, modes), "tm").astype(F32), axis=0)
    return (basis_rows, image)


def solution(mesh):
    return jax.shard_map(
        on_device,
        mesh=mesh,
        in_specs=(P("panel", "tm"), P(("panel", "tm"), None)),
        out_specs=(P("tm", None), P(("panel", "tm"), None)),
        check_vma=False,
    )
```

```python
import math

import jax
import jax.numpy as jnp
from jax import lax
from jax.experimental import pallas as pl
from jax.experimental.pallas import tpu as pltpu
from jax.sharding import PartitionSpec as P

F32 = jnp.float32
BF16 = jnp.bfloat16
GROUP = 8
PIECES = 6
IN_HBM = pl.BlockSpec(memory_space=pltpu.HBM)
IN_VMEM = pl.BlockSpec(memory_space=pltpu.VMEM)
ROOM = pltpu.CompilerParams(vmem_limit_bytes=32 << 20)


def fetch(pressures, held, arrived):
    rows = held.shape[0] // PIECES
    parts = [pl.ds(i * rows, rows) for i in range(PIECES)]
    copies = [pltpu.make_async_copy(pressures.at[r], held.at[r], arrived.at[i]) for i, r in enumerate(parts)]
    for copy in copies:
        copy.start()
    return list(zip(copies, parts))


def held_like(pressures):
    return [pltpu.VMEM(pressures.shape, pressures.dtype), pltpu.SemaphoreType.DMA((PIECES,))]


def own_core():
    return lax.rem(lax.axis_index("panel"), 2)


def projection_kernel(pressures, sketch, keep_ref, give_ref, held, arrived):
    total = None
    for copy, r in fetch(pressures, held, arrived):
        copy.wait()
        term = lax.dot_general(sketch[r, :], held[r, :], (((0,), (0,)), ((), ())), preferred_element_type=F32)
        total = term if total is None else total + term
    chips, rows, modes = keep_ref.shape
    y = total.T.reshape(chips, 2, rows, modes)
    first = own_core() == 0
    keep_ref[...] = jnp.where(first, y[:, 0], y[:, 1])
    give_ref[...] = jnp.where(first, y[:, 1], y[:, 0])


def projection(pressures, sketch, chips):
    samples = pressures.shape[1]
    modes = sketch.shape[1]
    half = jax.ShapeDtypeStruct((chips, samples // (2 * chips), modes), F32)
    return pl.pallas_call(
        projection_kernel,
        out_shape=(half, half),
        in_specs=[IN_HBM, IN_VMEM],
        out_specs=(IN_VMEM, IN_VMEM),
        scratch_shapes=held_like(pressures),
        compiler_params=ROOM,
    )(pressures, sketch)


def gram_kernel(mine, other, y_ref, copies_ref):
    first = own_core() == 0
    y_ref[:, 0] = jnp.where(first, mine[...], other[...])
    y_ref[:, 1] = jnp.where(first, other[...], mine[...])
    y = y_ref[...].reshape(-1, y_ref.shape[3])
    gram = lax.dot_general(
        y, y, (((0,), (0,)), ((), ())), precision=lax.Precision.HIGHEST, preferred_element_type=F32
    )
    half = copies_ref.shape[1]
    copies_ref[...] = jnp.broadcast_to(jnp.where(first, gram[:half], gram[half:])[None], copies_ref.shape)


def rows_and_gram(mine, other, copies):
    chips, rows, modes = mine.shape
    return pl.pallas_call(
        gram_kernel,
        out_shape=(
            jax.ShapeDtypeStruct((chips, 2, rows, modes), F32),
            jax.ShapeDtypeStruct((copies, modes // 2, modes), F32),
        ),
        in_specs=[IN_VMEM, IN_VMEM],
        out_specs=(IN_VMEM, IN_VMEM),
        compiler_params=ROOM,
    )(mine, other)


def inverse_factor(gram):
    n = gram.shape[0]
    groups = n // GROUP
    sub = lax.broadcasted_iota(jnp.int32, (GROUP, n), 0)
    lane = lax.broadcasted_iota(jnp.int32, (GROUP, n), 1)
    steps = range(GROUP)

    def wide(x):
        return jnp.broadcast_to(x, (GROUP, n))

    def columns_of(rows, k):
        return [wide(rows[:, k + m : k + m + 1]) for m in steps]

    left = [gram[GROUP * i : GROUP * (i + 1), :] for i in range(groups)]
    out = []
    for g in range(groups):
        k = GROUP * g
        inside = (lane >= k) & (lane < k + GROUP)
        columns = columns_of(left[g], k)
        block = {(m, l): columns[l][m : m + 1, :] for m in steps for l in range(m, GROUP)}
        over, scale = [], {}
        for m in steps:
            over.append(1.0 / block[m, m])
            for l in range(m + 1, GROUP):
                scale[m, l] = block[m, l] * over[m]
            for p in range(m + 1, GROUP):
                for l in range(p, GROUP):
                    block[p, l] = block[p, l] - scale[m, p] * block[m, l]
        start = jnp.where(inside, jnp.where(lane == sub + k, 1.0, 0.0), left[g])
        rows = []
        for m in steps:
            row = start[m : m + 1, :]
            for l in range(m):
                row = row - scale[l, m] * rows[l]
            rows.append(row)
        pivots = [wide(rows[m] * over[m]) for m in steps]
        scales = {key: wide(value) for key, value in scale.items()}
        for i in range(g + 1, groups):
            factors = []
            for m, f in enumerate(columns_of(left[i], k)):
                for l in range(m):
                    f = f - scales[l, m] * factors[l]
                factors.append(f)
            rest = jnp.where(inside, 0.0, left[i])
            for f, pivot in zip(factors, pivots):
                rest = rest - f * pivot
            left[i] = rest
        scaled = []
        for m in steps:
            root = lax.rsqrt(block[m, m])
            scaled.append(rows[m] * (root * (1.5 - 0.5 * block[m, m] * root * root)))
        out.append(jnp.where(lane < k + GROUP, jnp.concatenate(scaled, axis=0), 0.0))
    return out


def image_kernel(pressures, mine, other, y_ref, basis_ref, image_ref, held, arrived, inverse):
    arriving = fetch(pressures, held, arrived)
    first = own_core() == 0
    low = jnp.where(first, mine[...], other[...])
    high = jnp.where(first, other[...], mine[...])
    for i, rows in enumerate(inverse_factor(jnp.concatenate([low, high], axis=0))):
        inverse[GROUP * i : GROUP * (i + 1), :] = rows
    basis = lax.dot_general(
        y_ref[...],
        inverse[...],
        (((1,), (1,)), ((), ())),
        precision=lax.Precision.HIGHEST,
        preferred_element_type=F32,
    ).astype(BF16)
    basis_ref[...] = basis
    for copy, r in arriving:
        copy.wait()
        image_ref[r, :] = jnp.dot(held[r, :], basis, preferred_element_type=F32).astype(BF16)


def basis_and_image(pressures, mine, other, y_rows):
    panels = pressures.shape[0]
    samples, modes = y_rows.shape
    return pl.pallas_call(
        image_kernel,
        out_shape=(
            jax.ShapeDtypeStruct((samples, modes), BF16),
            jax.ShapeDtypeStruct((panels, modes), BF16),
        ),
        in_specs=[IN_HBM, IN_VMEM, IN_VMEM, IN_VMEM],
        out_specs=(IN_VMEM, IN_VMEM),
        scratch_shapes=[*held_like(pressures), pltpu.VMEM((modes, modes), F32)],
        compiler_params=ROOM,
    )(pressures, mine, other, y_rows)


def swap_cores(x):
    return lax.ppermute(x, "panel", [(i, i ^ 1) for i in range(lax.axis_size("panel"))])


def exchange(x, axis, groups=None):
    return lax.all_to_all(x, axis, 0, 0, axis_index_groups=groups)


def turns(across, side):
    along = [[], []]
    for p in range(across):
        at = [[p * side * side + x * side + y for y in range(side)] for x in range(side)]
        lines = [at, [list(column) for column in zip(*at)]]
        for turn in range(2):
            along[turn] += lines[(p + turn) % 2]
    return along


def copies_of(x, count):
    return jnp.broadcast_to(x[None], (count, *x.shape))


def on_device(pressures, sketch):
    pressures = pltpu.with_memory_space_constraint(pressures, pltpu.HBM)
    panels, samples = pressures.shape
    modes = sketch.shape[1]
    blocks = lax.axis_size("tm")
    across = lax.axis_size("panel")
    chips = across // 2
    side = math.isqrt(blocks)
    same_core = [[2 * z + c for z in range(chips)] for c in range(2)]
    one_way, other_way = turns(across, side)

    gathered = exchange(copies_of(sketch, blocks), "tm")
    keep, give = projection(pressures, gathered.reshape(panels, modes), chips)
    own = jnp.sum(exchange(keep + swap_cores(give), "panel", same_core), axis=0)
    mine = exchange(copies_of(own, chips), "panel", same_core)
    y_rows, half = rows_and_gram(mine, swap_cores(mine), side)
    line = jnp.sum(exchange(half, ("panel", "tm"), one_way), axis=0)
    half = jnp.sum(exchange(copies_of(line, side), ("panel", "tm"), other_way), axis=0)
    basis_rows, partial_image = basis_and_image(
        pressures, half, swap_cores(half), y_rows.reshape(samples, modes)
    )
    image = jnp.sum(exchange(partial_image.reshape(blocks, -1, modes), "tm").astype(F32), axis=0)
    return (basis_rows, image)


def solution(mesh):
    return jax.shard_map(
        on_device,
        mesh=mesh,
        in_specs=(P("panel", "tm"), P(("panel", "tm"), None)),
        out_specs=(P("tm", None), P(("panel", "tm"), None)),
        check_vma=False,
    )
```

```python
import math

import jax
import jax.numpy as jnp
from jax import lax
from jax.experimental import pallas as pl
from jax.experimental.pallas import tpu as pltpu
from jax.sharding import PartitionSpec as P

F32 = jnp.float32
BF16 = jnp.bfloat16
GROUP = 8
FOR_PROJECTION = 6
FOR_IMAGE = 3
IN_HBM = pl.BlockSpec(memory_space=pltpu.HBM)
IN_VMEM = pl.BlockSpec(memory_space=pltpu.VMEM)
ROOM = pltpu.CompilerParams(vmem_limit_bytes=32 << 20)


def fetch(pressures, held, arrived):
    pieces = arrived.shape[0]
    rows = held.shape[0] // pieces
    parts = [pl.ds(i * rows, rows) for i in range(pieces)]
    copies = [pltpu.make_async_copy(pressures.at[r], held.at[r], arrived.at[i]) for i, r in enumerate(parts)]
    for copy in copies:
        copy.start()
    return list(zip(copies, parts))


def held_like(pressures, pieces):
    return [pltpu.VMEM(pressures.shape, pressures.dtype), pltpu.SemaphoreType.DMA((pieces,))]


def own_core():
    return lax.rem(lax.axis_index("panel"), 2)


def projection_kernel(pressures, sketch, keep_ref, give_ref, held, arrived):
    total = None
    for copy, r in fetch(pressures, held, arrived):
        copy.wait()
        term = lax.dot_general(sketch[r, :], held[r, :], (((0,), (0,)), ((), ())), preferred_element_type=F32)
        total = term if total is None else total + term
    chips, rows, modes = keep_ref.shape
    y = total.T.reshape(chips, 2, rows, modes)
    first = own_core() == 0
    keep_ref[...] = jnp.where(first, y[:, 0], y[:, 1])
    give_ref[...] = jnp.where(first, y[:, 1], y[:, 0])


def projection(pressures, sketch, chips):
    samples = pressures.shape[1]
    modes = sketch.shape[1]
    half = jax.ShapeDtypeStruct((chips, samples // (2 * chips), modes), F32)
    return pl.pallas_call(
        projection_kernel,
        out_shape=(half, half),
        in_specs=[IN_HBM, IN_VMEM],
        out_specs=(IN_VMEM, IN_VMEM),
        scratch_shapes=held_like(pressures, FOR_PROJECTION),
        compiler_params=ROOM,
    )(pressures, sketch)


def gram_kernel(mine, other, y_ref, copies_ref):
    first = own_core() == 0
    y_ref[:, 0] = jnp.where(first, mine[...], other[...])
    y_ref[:, 1] = jnp.where(first, other[...], mine[...])
    y = y_ref[...].reshape(-1, y_ref.shape[3])
    gram = lax.dot_general(
        y, y, (((0,), (0,)), ((), ())), precision=lax.Precision.HIGHEST, preferred_element_type=F32
    )
    copies_ref[...] = jnp.broadcast_to(gram[None], copies_ref.shape)


def rows_and_gram(mine, other, copies):
    chips, rows, modes = mine.shape
    return pl.pallas_call(
        gram_kernel,
        out_shape=(
            jax.ShapeDtypeStruct((chips, 2, rows, modes), F32),
            jax.ShapeDtypeStruct((copies, modes, modes), F32),
        ),
        in_specs=[IN_VMEM, IN_VMEM],
        out_specs=(IN_VMEM, IN_VMEM),
        compiler_params=ROOM,
    )(mine, other)


def inverse_factor(gram):
    n = gram.shape[0]
    groups = n // GROUP
    sub = lax.broadcasted_iota(jnp.int32, (GROUP, n), 0)
    lane = lax.broadcasted_iota(jnp.int32, (GROUP, n), 1)
    steps = range(GROUP)

    def wide(x):
        return jnp.broadcast_to(x, (GROUP, n))

    def columns_of(rows, k):
        return [wide(rows[:, k + m : k + m + 1]) for m in steps]

    left = [gram[GROUP * i : GROUP * (i + 1), :] for i in range(groups)]
    out = []
    for g in range(groups):
        k = GROUP * g
        inside = (lane >= k) & (lane < k + GROUP)
        columns = columns_of(left[g], k)
        block = {(m, l): columns[l][m : m + 1, :] for m in steps for l in range(m, GROUP)}
        over, scale = [], {}
        for m in steps:
            over.append(1.0 / block[m, m])
            for l in range(m + 1, GROUP):
                scale[m, l] = block[m, l] * over[m]
            for p in range(m + 1, GROUP):
                for l in range(p, GROUP):
                    block[p, l] = block[p, l] - scale[m, p] * block[m, l]
        start = jnp.where(inside, jnp.where(lane == sub + k, 1.0, 0.0), left[g])
        rows = []
        for m in steps:
            row = start[m : m + 1, :]
            for l in range(m):
                row = row - scale[l, m] * rows[l]
            rows.append(row)
        pivots = [wide(rows[m] * over[m]) for m in steps]
        scales = {key: wide(value) for key, value in scale.items()}
        for i in range(g + 1, groups):
            factors = []
            for m, f in enumerate(columns_of(left[i], k)):
                for l in range(m):
                    f = f - scales[l, m] * factors[l]
                factors.append(f)
            rest = jnp.where(inside, 0.0, left[i])
            for f, pivot in zip(factors, pivots):
                rest = rest - f * pivot
            left[i] = rest
        scaled = []
        for m in steps:
            root = lax.rsqrt(block[m, m])
            scaled.append(rows[m] * (root * (1.5 - 0.5 * block[m, m] * root * root)))
        out.append(jnp.where(lane < k + GROUP, jnp.concatenate(scaled, axis=0), 0.0))
    return out


def image_kernel(pressures, gram_parts, y_ref, basis_ref, image_ref, held, arrived, inverse):
    arriving = fetch(pressures, held, arrived)
    for i, rows in enumerate(inverse_factor(jnp.sum(gram_parts[...], axis=0))):
        inverse[GROUP * i : GROUP * (i + 1), :] = rows
    basis = lax.dot_general(
        y_ref[...],
        inverse[...],
        (((1,), (1,)), ((), ())),
        precision=lax.Precision.HIGHEST,
        preferred_element_type=F32,
    ).astype(BF16)
    basis_ref[...] = basis
    for copy, r in arriving:
        copy.wait()
        image_ref[r, :] = jnp.dot(held[r, :], basis, preferred_element_type=F32).astype(BF16)


def basis_and_image(pressures, gram_parts, y_rows):
    panels = pressures.shape[0]
    samples, modes = y_rows.shape
    return pl.pallas_call(
        image_kernel,
        out_shape=(
            jax.ShapeDtypeStruct((samples, modes), BF16),
            jax.ShapeDtypeStruct((panels, modes), BF16),
        ),
        in_specs=[IN_HBM, IN_VMEM, IN_VMEM],
        out_specs=(IN_VMEM, IN_VMEM),
        scratch_shapes=[*held_like(pressures, FOR_IMAGE), pltpu.VMEM((modes, modes), F32)],
        compiler_params=ROOM,
    )(pressures, gram_parts, y_rows)


def swap_cores(x):
    return lax.ppermute(x, "panel", [(i, i ^ 1) for i in range(lax.axis_size("panel"))])


def exchange(x, axis, groups=None):
    return lax.all_to_all(x, axis, 0, 0, axis_index_groups=groups)


def on_device(pressures, sketch):
    pressures = pltpu.with_memory_space_constraint(pressures, pltpu.HBM)
    panels, samples = pressures.shape
    modes = sketch.shape[1]
    blocks = lax.axis_size("tm")
    chips = lax.axis_size("panel") // 2
    side = math.isqrt(blocks)
    same_x = [[x * side + y for y in range(side)] for x in range(side)]
    same_y = [[x * side + y for x in range(side)] for y in range(side)]
    same_core = [[2 * z + c for z in range(chips)] for c in range(2)]

    gathered = exchange(jnp.broadcast_to(sketch[None], (blocks, *sketch.shape)), "tm")
    keep, give = projection(pressures, gathered.reshape(panels, modes), chips)
    own = jnp.sum(exchange(keep + swap_cores(give), "panel", same_core), axis=0)
    mine = exchange(jnp.broadcast_to(own[None], (chips, *own.shape)), "panel", same_core)
    y_rows, gram = rows_and_gram(mine, swap_cores(mine), side)
    line = jnp.sum(exchange(gram, "tm", same_x), axis=0)
    gram_parts = exchange(jnp.broadcast_to(line[None], gram.shape), "tm", same_y)
    basis_rows, partial_image = basis_and_image(pressures, gram_parts, y_rows.reshape(samples, modes))
    image = jnp.sum(exchange(partial_image.reshape(blocks, -1, modes), "tm").astype(F32), axis=0)
    return (basis_rows, image)


def solution(mesh):
    return jax.shard_map(
        on_device,
        mesh=mesh,
        in_specs=(P("panel", "tm"), P(("panel", "tm"), None)),
        out_specs=(P("tm", None), P(("panel", "tm"), None)),
        check_vma=False,
    )
```

```python
import math

import jax
import jax.numpy as jnp
from jax import lax
from jax.experimental import pallas as pl
from jax.experimental.pallas import tpu as pltpu
from jax.sharding import PartitionSpec as P

F32 = jnp.float32
BF16 = jnp.bfloat16
GROUP = 8
FOR_PROJECTION = (4, 4, 3, 1)
FOR_IMAGE = (1, 1, 1)
IN_HBM = pl.BlockSpec(memory_space=pltpu.HBM)
IN_VMEM = pl.BlockSpec(memory_space=pltpu.VMEM)
ROOM = pltpu.CompilerParams(vmem_limit_bytes=32 << 20)


def fetch(pressures, held, arrived, shares):
    unit = held.shape[0] // sum(shares)
    parts = [pl.ds(sum(shares[:i]) * unit, share * unit) for i, share in enumerate(shares)]
    copies = [pltpu.make_async_copy(pressures.at[r], held.at[r], arrived.at[i]) for i, r in enumerate(parts)]
    for copy in copies:
        copy.start()
    return list(zip(copies, parts))


def held_like(pressures, shares):
    return [pltpu.VMEM(pressures.shape, pressures.dtype), pltpu.SemaphoreType.DMA((len(shares),))]


def own_core():
    return lax.rem(lax.axis_index("panel"), 2)


def projection_kernel(pressures, sketch, keep_ref, give_ref, held, arrived):
    total = None
    for copy, r in fetch(pressures, held, arrived, FOR_PROJECTION):
        copy.wait()
        term = lax.dot_general(sketch[r, :], held[r, :], (((0,), (0,)), ((), ())), preferred_element_type=F32)
        total = term if total is None else total + term
    chips, rows, modes = keep_ref.shape
    y = total.T.reshape(chips, 2, rows, modes)
    first = own_core() == 0
    keep_ref[...] = jnp.where(first, y[:, 0], y[:, 1])
    give_ref[...] = jnp.where(first, y[:, 1], y[:, 0])


def projection(pressures, sketch, chips):
    samples = pressures.shape[1]
    modes = sketch.shape[1]
    half = jax.ShapeDtypeStruct((chips, samples // (2 * chips), modes), F32)
    return pl.pallas_call(
        projection_kernel,
        out_shape=(half, half),
        in_specs=[IN_HBM, IN_VMEM],
        out_specs=(IN_VMEM, IN_VMEM),
        scratch_shapes=held_like(pressures, FOR_PROJECTION),
        compiler_params=ROOM,
    )(pressures, sketch)


def gram_kernel(mine, other, y_ref, copies_ref):
    first = own_core() == 0
    y_ref[:, 0] = jnp.where(first, mine[...], other[...])
    y_ref[:, 1] = jnp.where(first, other[...], mine[...])
    y = y_ref[...].reshape(-1, y_ref.shape[3])
    gram = lax.dot_general(
        y, y, (((0,), (0,)), ((), ())), precision=lax.Precision.HIGHEST, preferred_element_type=F32
    )
    copies_ref[...] = jnp.broadcast_to(gram[None], copies_ref.shape)


def rows_and_gram(mine, other, copies):
    chips, rows, modes = mine.shape
    return pl.pallas_call(
        gram_kernel,
        out_shape=(
            jax.ShapeDtypeStruct((chips, 2, rows, modes), F32),
            jax.ShapeDtypeStruct((copies, modes, modes), F32),
        ),
        in_specs=[IN_VMEM, IN_VMEM],
        out_specs=(IN_VMEM, IN_VMEM),
        compiler_params=ROOM,
    )(mine, other)


def inverse_factor(gram):
    n = gram.shape[0]
    groups = n // GROUP
    sub = lax.broadcasted_iota(jnp.int32, (GROUP, n), 0)
    lane = lax.broadcasted_iota(jnp.int32, (GROUP, n), 1)
    steps = range(GROUP)

    def wide(x):
        return jnp.broadcast_to(x, (GROUP, n))

    def columns_of(rows, k):
        return [wide(rows[:, k + m : k + m + 1]) for m in steps]

    left = [gram[GROUP * i : GROUP * (i + 1), :] for i in range(groups)]
    out = []
    for g in range(groups):
        k = GROUP * g
        inside = (lane >= k) & (lane < k + GROUP)
        columns = columns_of(left[g], k)
        block = {(m, l): columns[l][m : m + 1, :] for m in steps for l in range(m, GROUP)}
        over, scale = [], {}
        for m in steps:
            over.append(1.0 / block[m, m])
            for l in range(m + 1, GROUP):
                scale[m, l] = block[m, l] * over[m]
            for p in range(m + 1, GROUP):
                for l in range(p, GROUP):
                    block[p, l] = block[p, l] - scale[m, p] * block[m, l]
        start = jnp.where(inside, jnp.where(lane == sub + k, 1.0, 0.0), left[g])
        rows = []
        for m in steps:
            row = start[m : m + 1, :]
            for l in range(m):
                row = row - scale[l, m] * rows[l]
            rows.append(row)
        pivots = [wide(rows[m] * over[m]) for m in steps]
        scales = {key: wide(value) for key, value in scale.items()}
        for i in range(g + 1, groups):
            factors = []
            for m, f in enumerate(columns_of(left[i], k)):
                for l in range(m):
                    f = f - scales[l, m] * factors[l]
                factors.append(f)
            rest = jnp.where(inside, 0.0, left[i])
            for f, pivot in zip(factors, pivots):
                rest = rest - f * pivot
            left[i] = rest
        scaled = []
        for m in steps:
            root = lax.rsqrt(block[m, m])
            scaled.append(rows[m] * (root * (1.5 - 0.5 * block[m, m] * root * root)))
        out.append(jnp.where(lane < k + GROUP, jnp.concatenate(scaled, axis=0), 0.0))
    return out


def image_kernel(pressures, gram_parts, y_ref, basis_ref, image_ref, held, arrived, inverse):
    arriving = fetch(pressures, held, arrived, FOR_IMAGE)
    for i, rows in enumerate(inverse_factor(jnp.sum(gram_parts[...], axis=0))):
        inverse[GROUP * i : GROUP * (i + 1), :] = rows
    basis = lax.dot_general(
        y_ref[...],
        inverse[...],
        (((1,), (1,)), ((), ())),
        precision=lax.Precision.HIGHEST,
        preferred_element_type=F32,
    ).astype(BF16)
    basis_ref[...] = basis
    for copy, r in arriving:
        copy.wait()
        image_ref[r, :] = jnp.dot(held[r, :], basis, preferred_element_type=F32).astype(BF16)


def basis_and_image(pressures, gram_parts, y_rows):
    panels = pressures.shape[0]
    samples, modes = y_rows.shape
    return pl.pallas_call(
        image_kernel,
        out_shape=(
            jax.ShapeDtypeStruct((samples, modes), BF16),
            jax.ShapeDtypeStruct((panels, modes), BF16),
        ),
        in_specs=[IN_HBM, IN_VMEM, IN_VMEM],
        out_specs=(IN_VMEM, IN_VMEM),
        scratch_shapes=[*held_like(pressures, FOR_IMAGE), pltpu.VMEM((modes, modes), F32)],
        compiler_params=ROOM,
    )(pressures, gram_parts, y_rows)


def swap_cores(x):
    return lax.ppermute(x, "panel", [(i, i ^ 1) for i in range(lax.axis_size("panel"))])


def exchange(x, axis, groups=None):
    return lax.all_to_all(x, axis, 0, 0, axis_index_groups=groups)


def on_device(pressures, sketch):
    pressures = pltpu.with_memory_space_constraint(pressures, pltpu.HBM)
    panels, samples = pressures.shape
    modes = sketch.shape[1]
    blocks = lax.axis_size("tm")
    chips = lax.axis_size("panel") // 2
    side = math.isqrt(blocks)
    same_x = [[x * side + y for y in range(side)] for x in range(side)]
    same_y = [[x * side + y for x in range(side)] for y in range(side)]
    same_core = [[2 * z + c for z in range(chips)] for c in range(2)]

    gathered = exchange(jnp.broadcast_to(sketch[None], (blocks, *sketch.shape)), "tm")
    keep, give = projection(pressures, gathered.reshape(panels, modes), chips)
    own = jnp.sum(exchange(keep + swap_cores(give), "panel", same_core), axis=0)
    mine = exchange(jnp.broadcast_to(own[None], (chips, *own.shape)), "panel", same_core)
    y_rows, gram = rows_and_gram(mine, swap_cores(mine), side)
    line = jnp.sum(exchange(gram, "tm", same_x), axis=0)
    gram_parts = exchange(jnp.broadcast_to(line[None], gram.shape), "tm", same_y)
    basis_rows, partial_image = basis_and_image(pressures, gram_parts, y_rows.reshape(samples, modes))
    image = jnp.sum(exchange(partial_image.reshape(blocks, -1, modes), "tm").astype(F32), axis=0)
    return (basis_rows, image)


def solution(mesh):
    return jax.shard_map(
        on_device,
        mesh=mesh,
        in_specs=(P("panel", "tm"), P(("panel", "tm"), None)),
        out_specs=(P("tm", None), P(("panel", "tm"), None)),
        check_vma=False,
    )
```

```python
import math

import jax
import jax.numpy as jnp
from jax import lax
from jax.experimental import pallas as pl
from jax.experimental.pallas import tpu as pltpu
from jax.sharding import PartitionSpec as P

F32 = jnp.float32
BF16 = jnp.bfloat16
GROUP = 8
FOR_PROJECTION = 4
FOR_IMAGE = 3
IN_HBM = pl.BlockSpec(memory_space=pltpu.HBM)
IN_VMEM = pl.BlockSpec(memory_space=pltpu.VMEM)
ROOM = pltpu.CompilerParams(vmem_limit_bytes=32 << 20)


def fetch(pressures, held, arrived):
    pieces = arrived.shape[0]
    rows = held.shape[0] // pieces
    parts = [pl.ds(i * rows, rows) for i in range(pieces)]
    copies = [pltpu.make_async_copy(pressures.at[r], held.at[r], arrived.at[i]) for i, r in enumerate(parts)]
    for copy in copies:
        copy.start()
    return list(zip(copies, parts))


def held_like(pressures, pieces):
    return [pltpu.VMEM(pressures.shape, pressures.dtype), pltpu.SemaphoreType.DMA((pieces,))]


def own_core():
    return lax.rem(lax.axis_index("panel"), 2)


def projection_kernel(pressures, sketch, keep_ref, give_ref, held, arrived):
    total = None
    for copy, r in fetch(pressures, held, arrived):
        copy.wait()
        term = lax.dot_general(sketch[r, :], held[r, :], (((0,), (0,)), ((), ())), preferred_element_type=F32)
        total = term if total is None else total + term
    chips, rows, modes = keep_ref.shape
    y = total.T.reshape(chips, 2, rows, modes)
    first = own_core() == 0
    keep_ref[...] = jnp.where(first, y[:, 0], y[:, 1])
    give_ref[...] = jnp.where(first, y[:, 1], y[:, 0])


def projection(pressures, sketch, chips):
    samples = pressures.shape[1]
    modes = sketch.shape[1]
    half = jax.ShapeDtypeStruct((chips, samples // (2 * chips), modes), F32)
    return pl.pallas_call(
        projection_kernel,
        out_shape=(half, half),
        in_specs=[IN_HBM, IN_VMEM],
        out_specs=(IN_VMEM, IN_VMEM),
        scratch_shapes=held_like(pressures, FOR_PROJECTION),
        compiler_params=ROOM,
    )(pressures, sketch)


def gram_kernel(mine, other, y_ref, copies_ref):
    first = own_core() == 0
    y_ref[:, 0] = jnp.where(first, mine[...], other[...])
    y_ref[:, 1] = jnp.where(first, other[...], mine[...])
    y = y_ref[...].reshape(-1, y_ref.shape[3])
    gram = lax.dot_general(
        y, y, (((0,), (0,)), ((), ())), precision=lax.Precision.HIGHEST, preferred_element_type=F32
    )
    copies_ref[...] = jnp.broadcast_to(gram[None], copies_ref.shape)


def rows_and_gram(mine, other, copies):
    chips, rows, modes = mine.shape
    return pl.pallas_call(
        gram_kernel,
        out_shape=(
            jax.ShapeDtypeStruct((chips, 2, rows, modes), F32),
            jax.ShapeDtypeStruct((copies, modes, modes), F32),
        ),
        in_specs=[IN_VMEM, IN_VMEM],
        out_specs=(IN_VMEM, IN_VMEM),
        compiler_params=ROOM,
    )(mine, other)


def inverse_factor(gram):
    n = gram.shape[0]
    groups = n // GROUP
    sub = lax.broadcasted_iota(jnp.int32, (GROUP, n), 0)
    lane = lax.broadcasted_iota(jnp.int32, (GROUP, n), 1)
    steps = range(GROUP)

    def wide(x):
        return jnp.broadcast_to(x, (GROUP, n))

    def columns_of(rows, k):
        return [wide(rows[:, k + m : k + m + 1]) for m in steps]

    left = [gram[GROUP * i : GROUP * (i + 1), :] for i in range(groups)]
    out = []
    for g in range(groups):
        k = GROUP * g
        inside = (lane >= k) & (lane < k + GROUP)
        columns = columns_of(left[g], k)
        block = {(m, l): columns[l][m : m + 1, :] for m in steps for l in range(m, GROUP)}
        over, scale = [], {}
        for m in steps:
            over.append(1.0 / block[m, m])
            for l in range(m + 1, GROUP):
                scale[m, l] = block[m, l] * over[m]
            for p in range(m + 1, GROUP):
                for l in range(p, GROUP):
                    block[p, l] = block[p, l] - scale[m, p] * block[m, l]
        start = jnp.where(inside, jnp.where(lane == sub + k, 1.0, 0.0), left[g])
        rows = []
        for m in steps:
            row = start[m : m + 1, :]
            for l in range(m):
                row = row - scale[l, m] * rows[l]
            rows.append(row)
        pivots = [wide(rows[m] * over[m]) for m in steps]
        scales = {key: wide(value) for key, value in scale.items()}
        for i in range(g + 1, groups):
            factors = []
            for m, f in enumerate(columns_of(left[i], k)):
                for l in range(m):
                    f = f - scales[l, m] * factors[l]
                factors.append(f)
            rest = jnp.where(inside, 0.0, left[i])
            for f, pivot in zip(factors, pivots):
                rest = rest - f * pivot
            left[i] = rest
        scaled = []
        for m in steps:
            root = lax.rsqrt(block[m, m])
            scaled.append(rows[m] * (root * (1.5 - 0.5 * block[m, m] * root * root)))
        out.append(jnp.where(lane < k + GROUP, jnp.concatenate(scaled, axis=0), 0.0))
    return out


def image_kernel(pressures, gram_parts, y_ref, basis_ref, image_ref, held, arrived, inverse):
    arriving = fetch(pressures, held, arrived)
    for i, rows in enumerate(inverse_factor(jnp.sum(gram_parts[...], axis=0))):
        inverse[GROUP * i : GROUP * (i + 1), :] = rows
    basis = lax.dot_general(
        y_ref[...],
        inverse[...],
        (((1,), (1,)), ((), ())),
        precision=lax.Precision.HIGHEST,
        preferred_element_type=F32,
    ).astype(BF16)
    basis_ref[...] = basis
    for copy, r in arriving:
        copy.wait()
        image_ref[r, :] = jnp.dot(held[r, :], basis, preferred_element_type=F32).astype(BF16)


def basis_and_image(pressures, gram_parts, y_rows):
    panels = pressures.shape[0]
    samples, modes = y_rows.shape
    return pl.pallas_call(
        image_kernel,
        out_shape=(
            jax.ShapeDtypeStruct((samples, modes), BF16),
            jax.ShapeDtypeStruct((panels, modes), BF16),
        ),
        in_specs=[IN_HBM, IN_VMEM, IN_VMEM],
        out_specs=(IN_VMEM, IN_VMEM),
        scratch_shapes=[*held_like(pressures, FOR_IMAGE), pltpu.VMEM((modes, modes), F32)],
        compiler_params=ROOM,
    )(pressures, gram_parts, y_rows)


def swap_cores(x):
    return lax.ppermute(x, "panel", [(i, i ^ 1) for i in range(lax.axis_size("panel"))])


def exchange(x, axis, groups=None):
    return lax.all_to_all(x, axis, 0, 0, axis_index_groups=groups)


def on_device(pressures, sketch):
    pressures = pltpu.with_memory_space_constraint(pressures, pltpu.HBM)
    panels, samples = pressures.shape
    modes = sketch.shape[1]
    blocks = lax.axis_size("tm")
    chips = lax.axis_size("panel") // 2
    side = math.isqrt(blocks)
    same_x = [[x * side + y for y in range(side)] for x in range(side)]
    same_y = [[x * side + y for x in range(side)] for y in range(side)]
    same_core = [[2 * z + c for z in range(chips)] for c in range(2)]

    gathered = exchange(jnp.broadcast_to(sketch[None], (blocks, *sketch.shape)), "tm")
    keep, give = projection(pressures, gathered.reshape(panels, modes), chips)
    own = jnp.sum(exchange(keep + swap_cores(give), "panel", same_core), axis=0)
    mine = exchange(jnp.broadcast_to(own[None], (chips, *own.shape)), "panel", same_core)
    y_rows, gram = rows_and_gram(mine, swap_cores(mine), side)
    line = jnp.sum(exchange(gram, "tm", same_x), axis=0)
    gram_parts = exchange(jnp.broadcast_to(line[None], gram.shape), "tm", same_y)
    basis_rows, partial_image = basis_and_image(pressures, gram_parts, y_rows.reshape(samples, modes))
    image = jnp.sum(exchange(partial_image.reshape(blocks, -1, modes), "tm").astype(F32), axis=0)
    return (basis_rows, image)


def solution(mesh):
    return jax.shard_map(
        on_device,
        mesh=mesh,
        in_specs=(P("panel", "tm"), P(("panel", "tm"), None)),
        out_specs=(P("tm", None), P(("panel", "tm"), None)),
        check_vma=False,
    )
```
